32 devices in a mesh: groups: 2 (over x), dp: 16 (over z, y, core).
Axes of the slice: x: 2, y: 2, z: 4, core: 2. Of those that a mesh axis runs over, the one named last changes fastest.
Arguments:
- latents: bfloat16 [256, 16, 16, 384], P(('groups', 'dp')), parts along dimension 0, may hold values from -6 to 6
- base_features: bfloat16 [256, 16, 16, 384], P(('groups', 'dp')), parts along dimension 0, may hold values from -6 to 6
- cotangent: bfloat16 [256, 16, 16, 384], P(('groups', 'dp')), parts along dimension 0, may hold values from -0.032958984 to 0.032958984
- class_ids: int32 [256], P(('groups', 'dp')), parts along dimension 0, may hold values from 0 to 999
- timesteps: int32 [256], P(('groups', 'dp')), parts along dimension 0, may hold values from 0 to 999
- class_table: float32 [1000, 384], replicated, may hold values from -6 to 6
- control_weight: bfloat16 [3456, 384], P('dp'), may hold values from -0.109375 to 0.109375
- join_weight: bfloat16 [384, 384], P('dp'), may hold values from -0.3125 to 0.3125
- decoder_weight: bfloat16 [384, 384], replicated, may hold values from -0.3125 to 0.3125
Outputs:
- decoded: bfloat16 [256, 16, 16, 384], P(('groups', 'dp')), parts along dimension 0
- control_grad: float32 [6912, 384], P(('groups', 'dp')), parts along dimension 0
- join_grad: float32 [768, 384], P(('groups', 'dp')), parts along dimension 0
The draws below stay inside these ranges and needn't reach their ends.
There are 2 independent parts, one for each index of `groups`. The reference program is written for one: setup_inputs(seed, part) draws one part's arguments, and reference() takes and returns one part's arrays. A program takes and returns all parts, laid end to end along the dimension named above; an argument that names none is the same for every part. Nothing has to cross between parts.
All inputs are finite; a program needn't handle non-finite values.
Results may differ from the reference program's by a relative error of at most 0.0062.
Values may be sent and summed in bfloat16 or wider, within the bound.
A program may use at most 128 MiB of HBM per device.

```python
import math
import jax
import jax.numpy as jnp
from jax import lax

C = 384
CLASSES = 1000
NORM_GROUPS = 32
TSTEPS = 1000
SIDE = 16
SAMP_DEV = 8
BATCH = 128
N_DP = 16


def place_ends(entries, key, low, largest):
    longest = entries.shape.index(max(entries.shape))
    spots = []
    for shift in (0, 1):
        where = [jax.random.randint(jax.random.fold_in(key, axis), (), 0, length) for axis, length in enumerate(entries.shape)]
        where[longest] = (where[longest] + shift) % entries.shape[longest]
        spots.append(tuple(where))
    return entries.at[spots[0]].set(low).at[spots[1]].set(largest)


def block_scale(rng, dims, cuts, smallest, largest):
    level, own = 1.0, jax.random.fold_in(rng, 6)
    for dim, blocks in cuts:
        heights = jnp.exp(jax.random.uniform(jax.random.fold_in(own, dim), (blocks,), jnp.float32, smallest / len(cuts), largest / len(cuts)))
        level = level * jnp.repeat(heights, dims[dim] // blocks).reshape([-1 if axis == dim else 1 for axis in range(len(dims))])
    return level


def centred(rng, dims, deviation, most, cuts=(), held_as=jnp.bfloat16):
    entries = jax.random.normal(rng, dims, jnp.float32) * deviation
    if len(cuts) > 0:
        entries = block_scale(rng, dims, cuts, -0.22, 0.18) * entries
    return jnp.clip(entries, min=-most, max=most).astype(held_as)


def setup_inputs(seed: int = 0, part: int = 0) -> dict:
    streams_of = jax.random.split(jax.random.key(seed), 10)
    part_splits = jax.random.split(jax.random.fold_in(streams_of[9], part), 10)
    latents = centred(part_splits[0], (BATCH, SIDE, SIDE, C), 1.0, 6.0, ((0, 16),))
    base_features = centred(part_splits[1], (BATCH, SIDE, SIDE, C), 1.0, 6.0, ((0, 16),))
    cotangent = centred(part_splits[2], (BATCH, SIDE, SIDE, C), ((SAMP_DEV * N_DP * SIDE * SIDE) ** -0.5), 0.032958984, ((0, 16),))
    class_ids = place_ends(jax.random.randint(part_splits[3], (BATCH,), 0, CLASSES), jax.random.fold_in(part_splits[3], 1), 0, CLASSES - 1).astype(jnp.int32)
    timesteps = place_ends(jax.random.randint(part_splits[4], (BATCH,), 0, TSTEPS), jax.random.fold_in(part_splits[4], 1), 0, TSTEPS - 1).astype(jnp.int32)
    class_table = centred(streams_of[5], (CLASSES, C), 1.0, 6.0, (), jnp.float32)
    control_weight = centred(streams_of[6], (9 * C, C), (9 * C) ** -0.5, 0.109375, ((0, 16),))
    join_weight = centred(streams_of[7], (C, C), C ** -0.5, 0.3125, ((0, 16),))
    decoder_weight = centred(streams_of[8], (C, C), C ** -0.5, 0.3125)
    return {"latents": latents, "base_features": base_features, "cotangent": cotangent, "class_ids": class_ids, "timesteps": timesteps, "class_table": class_table, "control_weight": control_weight, "join_weight": join_weight, "decoder_weight": decoder_weight}


def time_features(steps_in, width):
    half = width // 2
    freq = jnp.exp(-math.log(10000.0) * jnp.arange(half, dtype=jnp.float32) / half)
    angle = steps_in.astype(jnp.float32)[:, None] * freq[None, :]
    return jnp.concatenate([jnp.cos(angle), jnp.sin(angle)], axis=1)

def silu_slope(value):
    sig = jax.nn.sigmoid(value)
    return sig * (1.0 + value * (1.0 - sig))

def group_normalize(hsum, groups):
    count, side, _, width = hsum.shape
    grouped = hsum.reshape(count, side, side, groups, width // groups)
    mean = lax.optimization_barrier(jnp.mean(grouped, axis=(1, 2, 4), keepdims=True))
    var = lax.optimization_barrier(jnp.mean((grouped - mean) ** 2, axis=(1, 2, 4), keepdims=True))
    return ((grouped - mean) / jnp.sqrt(var + 1e-05)).reshape(hsum.shape).astype(jnp.bfloat16)

def patch_rows(normed):
    count, side, _, width = normed.shape
    padded = jnp.pad(normed, ((0, 0), (1, 1), (1, 1), (0, 0)))
    shifted = [padded[:, ty:ty + side, tx:tx + side, :] for ty in range(3) for tx in range(3)]
    return jnp.concatenate(shifted, axis=3).reshape(count * side * side, 9 * width)

def one_block(latent, base, cot, classes, tsteps, class_table, control_weight, join_weight, decoder_weight):
    count, side, _, width = latent.shape
    embed = class_table[classes]
    hsum = latent.astype(jnp.float32) + (embed + time_features(tsteps, width))[:, None, None, :]
    normed = group_normalize(hsum, NORM_GROUPS)
    patches = patch_rows(normed)
    conv = jnp.dot(patches, control_weight, preferred_element_type=jnp.float32)
    act = jax.nn.silu(conv).astype(jnp.bfloat16)
    joined = base.reshape(-1, width).astype(jnp.float32) + jnp.dot(act, join_weight, preferred_element_type=jnp.float32)
    mixed = jax.nn.silu(joined).astype(jnp.bfloat16)
    decoded = jnp.dot(mixed, decoder_weight, preferred_element_type=jnp.float32).astype(jnp.bfloat16)
    cot_rows = cot.reshape(-1, width)
    dmixed = jnp.dot(cot_rows, decoder_weight.T, preferred_element_type=jnp.float32)
    djoin = (dmixed * silu_slope(joined)).astype(jnp.bfloat16)
    join_term = jnp.dot(act.T, djoin, preferred_element_type=jnp.float32)
    dact = jnp.dot(djoin, join_weight.T, preferred_element_type=jnp.float32)
    dconv = (dact * silu_slope(conv)).astype(jnp.bfloat16)
    control_term = jnp.dot(patches.T, dconv, preferred_element_type=jnp.float32)
    return (decoded.reshape(latent.shape), control_term, join_term)

def reference(latents, base_features, cotangent, class_ids, timesteps, class_table, control_weight, join_weight, decoder_weight):
    width = latents.shape[3]
    blocks = N_DP

    def split(arr):
        return arr.reshape((blocks, arr.shape[0] // blocks) + arr.shape[1:])

    def step(carry, items):
        latent, base, cot, classes, tsteps = items
        decoded, control_term, join_term = one_block(latent, base, cot, classes, tsteps, class_table, control_weight, join_weight, decoder_weight)
        return ((carry[0] + control_term, carry[1] + join_term), decoded)
    init = (jnp.zeros((9 * width, width), jnp.float32), jnp.zeros((width, width), jnp.float32))
    grads, decoded = lax.scan(step, init, (split(latents), split(base_features), split(cotangent), split(class_ids), split(timesteps)))
    return (decoded.reshape(latents.shape), grads[0], grads[1])
```

```python
import functools
import math

import jax
import jax.numpy as jnp
from jax import lax
from jax.experimental import pallas as pl
from jax.experimental.pallas import tpu as pltpu
from jax.sharding import PartitionSpec as P

NORM_GROUPS = 32
MESH = pl.DeviceIdType.MESH
F32 = jnp.float32
BF16 = jnp.bfloat16
VMEM_LIMIT = 60000 * 1024


def time_features(steps_in, width):
    half = width // 2
    freq = jnp.exp(-math.log(10000.0) * jnp.arange(half, dtype=jnp.float32) / half)
    angle = steps_in.astype(jnp.float32)[:, None] * freq[None, :]
    return jnp.concatenate([jnp.cos(angle), jnp.sin(angle)], axis=1)


def silu_slope(value):
    sig = jax.nn.sigmoid(value)
    return sig * (1.0 + value * (1.0 - sig))


def dp_index(spot, core):
    y = spot // 4
    z = spot + y * (7 - 2 * spot)
    return z * 4 + y * 2 + core


def ring_place():
    me = lax.axis_index("dp")
    z, y, core = me // 4, (me // 2) % 2, me % 2
    return me, z + y * (7 - 2 * z), core


def greet(partners):
    barrier = pltpu.get_barrier_semaphore()
    for partner in partners:
        pl.semaphore_signal(barrier, inc=1, device_id={"dp": partner}, device_id_type=MESH)
    pl.semaphore_wait(barrier, len(partners))


def remote(src, dst, sends, recvs, place, partner):
    return pltpu.make_async_remote_copy(
        src_ref=src,
        dst_ref=dst,
        send_sem=sends.at[place],
        recv_sem=recvs.at[place],
        device_id={"dp": partner},
        device_id_type=MESH,
    )


def gather_kernel(control_ref, join_ref, control_out, join_out, own_sem, sends, recvs):
    me, spot, core = ring_place()
    ahead = dp_index((spot + 1) % 8, core)
    behind = dp_index((spot + 7) % 8, core)
    twin = dp_index(spot, 1 - core)
    greet((ahead, behind, twin))
    started = []

    def send(source, block, kind, partner):
        for which, (own, out) in enumerate(((control_ref, control_out), (join_ref, join_out))):
            copy = remote(
                own if source else out.at[block],
                out.at[block],
                sends,
                recvs,
                which * 15 + kind,
                partner,
            )
            copy.start()
            started.append(copy)

    def arrived(block, kind):
        for which, out in enumerate((control_out, join_out)):
            remote(
                out.at[block], out.at[block], sends, recvs, which * 15 + kind, twin
            ).wait_recv()

    send(True, me, 0, ahead)
    send(True, me, 4, behind)
    send(True, me, 7, twin)
    local = [
        pltpu.make_async_copy(own, out.at[me], own_sem.at[which])
        for which, (own, out) in enumerate(((control_ref, control_out), (join_ref, join_out)))
    ]
    for copy in local:
        copy.start()
    for step in range(4):
        block = dp_index((spot + 7 - step) % 8, core)
        arrived(block, step)
        if step < 3:
            send(False, block, step + 1, ahead)
        send(False, block, 8 + step, twin)
        if step < 3:
            block = dp_index((spot + 1 + step) % 8, core)
            arrived(block, 4 + step)
            if step < 2:
                send(False, block, 5 + step, behind)
            send(False, block, 12 + step, twin)
    for copy in local:
        copy.wait()
    arrived(dp_index(spot, 1 - core), 7)
    for step in range(4):
        arrived(dp_index((spot + 7 - step) % 8, 1 - core), 8 + step)
    for step in range(3):
        arrived(dp_index((spot + 1 + step) % 8, 1 - core), 12 + step)
    for copy in started:
        copy.wait_send()


def gather_weights(control, join):
    return pl.pallas_call(
        gather_kernel,
        out_shape=(
            jax.ShapeDtypeStruct((16,) + control.shape, BF16),
            jax.ShapeDtypeStruct((16,) + join.shape, BF16),
        ),
        in_specs=[pl.BlockSpec(memory_space=pl.ANY)] * 2,
        out_specs=[pl.BlockSpec(memory_space=pl.ANY)] * 2,
        scratch_shapes=[
            pltpu.SemaphoreType.DMA((2,)),
            pltpu.SemaphoreType.DMA((30,)),
            pltpu.SemaphoreType.DMA((30,)),
        ],
        compiler_params=pltpu.CompilerParams(collective_id=0, has_side_effects=True),
        name="gather_weights",
    )(control, join)


def scatter_kernel(
    g_ref, j_ref, g_out, j_out,
    g_twin, j_twin, g_send, j_send, g_recv, j_recv, sends, recvs,
):
    me, spot, core = ring_place()
    ahead = dp_index((spot + 1) % 8, core)
    behind = dp_index((spot + 7) % 8, core)
    twin = dp_index(spot, 1 - core)
    greet((ahead, behind, twin))
    arrays = ((g_ref, g_twin, g_send, g_recv, g_out), (j_ref, j_twin, j_send, j_recv, j_out))
    order = (4, 5, 3, 6, 2, 7, 1, 0)
    started = []
    for k in order:
        for which, (part, held, _, _, _) in enumerate(arrays):
            copy = remote(
                part.at[dp_index((spot + k) % 8, 1 - core)],
                held.at[k], sends, recvs, which * 15 + 7 + k, twin,
            )
            copy.start()
            started.append(copy)

    def pair_sum(which, k):
        part, held, _, _, _ = arrays[which]
        remote(held.at[k], held.at[k], sends, recvs, which * 15 + 7 + k, twin).wait_recv()
        return part[dp_index((spot + k) % 8, core)].astype(F32) + held[k].astype(F32)

    def got(which, place):
        back = arrays[which][3]
        remote(back.at[place], back.at[place], sends, recvs, which * 15 + place, twin).wait_recv()
        return back[place].astype(F32)

    def hop(which, place, value, partner):
        _, _, out, back, _ = arrays[which]
        out[place] = value.astype(BF16)
        copy = remote(out.at[place], back.at[place], sends, recvs, which * 15 + place, partner)
        copy.start()
        started.append(copy)

    for step in range(4):
        for which in range(2):
            value = pair_sum(which, 4 - step)
            if step > 0:
                value = value + got(which, step - 1)
            hop(which, step, value, ahead)
        if step < 3:
            for which in range(2):
                value = pair_sum(which, 5 + step)
                if step > 0:
                    value = value + got(which, 4 + step - 1)
                hop(which, 4 + step, value, behind)
    for which in range(2):
        arrays[which][4][...] = pair_sum(which, 0) + got(which, 6) + got(which, 3)
    for copy in started:
        copy.wait_send()


def scatter_sums(control, join):
    shapes = [control.shape[1:], join.shape[1:]]
    return pl.pallas_call(
        scatter_kernel,
        out_shape=tuple(jax.ShapeDtypeStruct(shape, F32) for shape in shapes),
        in_specs=[pl.BlockSpec(memory_space=pltpu.VMEM)] * 2,
        out_specs=[pl.BlockSpec(memory_space=pltpu.VMEM)] * 2,
        scratch_shapes=[
            pltpu.VMEM((slots,) + shape, BF16) for slots in (8, 7, 7) for shape in shapes
        ]
        + [pltpu.SemaphoreType.DMA((30,)), pltpu.SemaphoreType.DMA((30,))],
        compiler_params=pltpu.CompilerParams(
            collective_id=1, has_side_effects=True, vmem_limit_bytes=VMEM_LIMIT
        ),
        name="scatter_sums",
    )(control, join)


def shifted_columns(value, step, side):
    rows = value.shape[0]
    spot = lax.broadcasted_iota(jnp.int32, value.shape, 0) % side
    if step > 0:
        return jnp.where(spot == side - 1, 0.0, pltpu.roll(value, rows - 1, 0))
    return jnp.where(spot == 0, 0.0, pltpu.roll(value, 1, 0))


def step_kernel(
    lat_ref, base_ref, cot_ref, embed_ref, control_ref, join_ref, decoder_ref,
    decoded_ref, control_grad_ref, join_grad_ref,
    taps_ref, shifts_ref, flipped_ref, join_sum_ref, mean_ref, root_ref,
    *, side, groups, batch,
):
    count, pixels, width = lat_ref.shape
    per = width // groups
    lane = lambda axis: lax.broadcasted_iota(jnp.int32, (width, width), axis)
    low = lane(0) * groups // width * per
    same = ((lane(1) >= low) & (lane(1) < low + per)).astype(F32)
    spread = functools.partial(
        jnp.dot, precision=lax.Precision.HIGHEST, preferred_element_type=F32
    )
    scale = 1.0 / (pixels * per)
    dot = functools.partial(lax.dot_general, preferred_element_type=F32)

    edge = jnp.zeros((count, side, 3 * width), BF16)
    for ref in (taps_ref, shifts_ref):
        ref[:, :side, :] = edge
        ref[:, side + pixels :, :] = edge

    def hsum(s):
        return lat_ref[s].astype(F32) + embed_ref[pl.ds(s, 1), :]

    def add_up(s, carry):
        mean_ref[pl.ds(s, 1), :] = jnp.sum(hsum(s), axis=0, keepdims=True)
        return carry

    def add_squares(s, carry):
        diff = hsum(s) - mean_ref[pl.ds(s, 1), :]
        root_ref[pl.ds(s, 1), :] = jnp.sum(diff * diff, axis=0, keepdims=True)
        return carry

    lax.fori_loop(0, count, add_up, 0)
    mean_ref[...] = spread(mean_ref[...], same) * scale
    lax.fori_loop(0, count, add_squares, 0)
    root_ref[...] = 1.0 / jnp.sqrt(spread(root_ref[...], same) * scale + 1e-05)

    def normalize(s, carry):
        normed = (hsum(s) - mean_ref[pl.ds(s, 1), :]) * root_ref[pl.ds(s, 1), :]
        inner = pl.ds(side, pixels)
        taps_ref[s, inner, :width] = shifted_columns(normed, -1, side).astype(BF16)
        taps_ref[s, inner, width : 2 * width] = normed.astype(BF16)
        taps_ref[s, inner, 2 * width :] = shifted_columns(normed, 1, side).astype(BF16)
        flipped_ref[:, pl.ds(pl.multiple_of(s * pixels, pixels), pixels)] = normed.T.astype(BF16)
        return carry

    lax.fori_loop(0, count, normalize, 0)
    join_sum_ref[...] = jnp.zeros_like(join_sum_ref)
    wide = 3 * width
    rows = batch * pixels

    def through(c, carry):
        some = pl.ds(c * batch, batch)
        conv = None
        for ty in range(3):
            term = jnp.dot(
                taps_ref[some, pl.ds(ty * side, pixels), :].reshape(rows, wide),
                control_ref[pl.ds(ty * wide, wide), :],
                preferred_element_type=F32,
            )
            conv = term if conv is None else conv + term
        sig = jax.nn.sigmoid(conv)
        act = (conv * sig).astype(BF16)
        slope = sig * (1.0 + conv * (1.0 - sig))
        joined = base_ref[some].reshape(rows, width).astype(F32) + jnp.dot(
            act, join_ref[...], preferred_element_type=F32
        )
        sig = jax.nn.sigmoid(joined)
        mixed = (joined * sig).astype(BF16)
        decoded = jnp.dot(mixed, decoder_ref[...], preferred_element_type=F32)
        decoded_ref[some] = decoded.astype(BF16).reshape(batch, pixels, width)
        dmixed = dot(cot_ref[some].reshape(rows, width), decoder_ref[...], (((1,), (1,)), ((), ())))
        djoin = (dmixed * (sig * (1.0 + joined * (1.0 - sig)))).astype(BF16)
        join_sum_ref[...] += dot(act, djoin, (((0,), (0,)), ((), ())))
        dconv = dot(djoin, join_ref[...], (((1,), (1,)), ((), ()))) * slope
        shape = (batch, pixels, width)
        inner = pl.ds(side, pixels)
        shifts_ref[some, inner, :width] = (
            shifted_columns(dconv, 1, side).astype(BF16).reshape(shape)
        )
        shifts_ref[some, inner, width : 2 * width] = dconv.astype(BF16).reshape(shape)
        shifts_ref[some, inner, 2 * width :] = (
            shifted_columns(dconv, -1, side).astype(BF16).reshape(shape)
        )
        return carry

    lax.fori_loop(0, count // batch, through, 0)
    join_grad_ref[...] = join_sum_ref[...].astype(join_grad_ref.dtype)
    for ty in range(3):
        grads = jnp.dot(
            flipped_ref[...],
            shifts_ref[:, pl.ds((2 - ty) * side, pixels), :].reshape(count * pixels, wide),
            preferred_element_type=F32,
        )
        for tx in range(3):
            control_grad_ref[pl.ds((ty * 3 + tx) * width, width), :] = grads[
                :, tx * width : (tx + 1) * width
            ].astype(control_grad_ref.dtype)


def local_step(lat, base, cot, embed, control, join, decoder, side, grad_dtype):
    count, pixels, width = lat.shape
    batch = 2 if count % 2 == 0 else 1
    flops = 2 * count * pixels * width * width * 23
    return pl.pallas_call(
        functools.partial(step_kernel, side=side, groups=NORM_GROUPS, batch=batch),
        out_shape=(
            jax.ShapeDtypeStruct(lat.shape, BF16),
            jax.ShapeDtypeStruct(control.shape, grad_dtype),
            jax.ShapeDtypeStruct(join.shape, grad_dtype),
        ),
        in_specs=[pl.BlockSpec(memory_space=pltpu.VMEM)] * 7,
        out_specs=[pl.BlockSpec(memory_space=pltpu.VMEM)] * 3,
        scratch_shapes=[
            pltpu.VMEM((count, pixels + 2 * side, 3 * width), BF16),
            pltpu.VMEM((count, pixels + 2 * side, 3 * width), BF16),
            pltpu.VMEM((width, count * pixels), BF16),
            pltpu.VMEM((width, width), F32),
            pltpu.VMEM((count, width), F32),
            pltpu.VMEM((count, width), F32),
        ],
        compiler_params=pltpu.CompilerParams(vmem_limit_bytes=VMEM_LIMIT),
        cost_estimate=pl.CostEstimate(
            flops=flops, bytes_accessed=16 * 2**20, transcendentals=4 * lat.size
        ),
        name="local_step",
    )(lat, base, cot, embed, control, join, decoder)


def on_device(
    ringed, latents, base_features, cotangent, class_ids, timesteps,
    class_table, control_weight, join_weight, decoder_weight,
):
    count, side, _, width = latents.shape
    flat = lambda array: array.reshape(count, side * side, width)
    embed = class_table.at[class_ids].get(mode="promise_in_bounds") + time_features(
        timesteps, width
    )
    if ringed:
        control_full, join_full = gather_weights(control_weight, join_weight)
    else:
        control_full, join_full = (
            lax.all_gather(weight, "dp", axis=0, tiled=True)
            for weight in (control_weight, join_weight)
        )
    decoded, control_part, join_part = local_step(
        flat(latents),
        flat(base_features),
        flat(cotangent),
        embed,
        control_full.reshape(-1, width),
        join_full.reshape(-1, width),
        decoder_weight,
        side,
        BF16 if ringed else F32,
    )
    if ringed:
        blocks = lambda array: array.reshape(16, -1, width)
        control_grad, join_grad = scatter_sums(blocks(control_part), blocks(join_part))
    else:
        control_grad, join_grad = (
            lax.psum_scatter(part, "dp", scatter_dimension=0, tiled=True)
            for part in (control_part, join_part)
        )
    return decoded.reshape(latents.shape), control_grad, join_grad


def solution(mesh):
    rows = P(("groups", "dp"), None)
    maps = P(("groups", "dp"), None, None, None)
    each = P(("groups", "dp"))
    split = P("dp", None)
    ringed = mesh.shape["dp"] == 16
    return jax.shard_map(
        functools.partial(on_device, ringed),
        mesh=mesh,
        in_specs=(maps, maps, maps, each, each, P(), split, split, P()),
        out_specs=(maps, rows, rows),
        check_vma=False,
    )
```

```python
import functools
import math

import jax
import jax.numpy as jnp
from jax import lax
from jax.experimental import pallas as pl
from jax.experimental.pallas import tpu as pltpu
from jax.sharding import PartitionSpec as P

NORM_GROUPS = 32
MESH = pl.DeviceIdType.MESH
F32 = jnp.float32
BF16 = jnp.bfloat16
VMEM_LIMIT = 60000 * 1024


def time_features(steps_in, width):
    half = width // 2
    freq = jnp.exp(-math.log(10000.0) * jnp.arange(half, dtype=jnp.float32) / half)
    angle = steps_in.astype(jnp.float32)[:, None] * freq[None, :]
    return jnp.concatenate([jnp.cos(angle), jnp.sin(angle)], axis=1)


def silu_slope(value):
    sig = jax.nn.sigmoid(value)
    return sig * (1.0 + value * (1.0 - sig))


def dp_index(spot, core):
    y = spot // 4
    z = spot + y * (7 - 2 * spot)
    return z * 4 + y * 2 + core


def ring_place():
    me = lax.axis_index("dp")
    z, y, core = me // 4, (me // 2) % 2, me % 2
    return me, z + y * (7 - 2 * z), core


def greet(partners):
    barrier = pltpu.get_barrier_semaphore()
    for partner in partners:
        pl.semaphore_signal(barrier, inc=1, device_id={"dp": partner}, device_id_type=MESH)
    pl.semaphore_wait(barrier, len(partners))


def remote(src, dst, sends, recvs, place, partner):
    return pltpu.make_async_remote_copy(
        src_ref=src,
        dst_ref=dst,
        send_sem=sends.at[place],
        recv_sem=recvs.at[place],
        device_id={"dp": partner},
        device_id_type=MESH,
    )


def shifted_columns(value, step, side):
    rows = value.shape[0]
    spot = lax.broadcasted_iota(jnp.int32, value.shape, 0) % side
    if step > 0:
        return jnp.where(spot == side - 1, 0.0, pltpu.roll(value, rows - 1, 0))
    return jnp.where(spot == 0, 0.0, pltpu.roll(value, 1, 0))


CUTS = ((0, 256), (256, 128))


def math_parts(
    lat_ref, base_ref, cot_ref, embed_ref, control_ref, join_ref, decoder_ref, decoded_ref,
    taps_ref, shifts_ref, flipped_ref, join_sum_ref, mean_ref, root_ref, *, side, groups,
):
    count, pixels, width = lat_ref.shape
    batch = 2 if count % 2 == 0 else 1
    per = width // groups
    spread = functools.partial(
        jnp.dot, precision=lax.Precision.HIGHEST, preferred_element_type=F32
    )
    scale = 1.0 / (pixels * per)
    dot = functools.partial(lax.dot_general, preferred_element_type=F32)
    wide = 3 * width
    rows = batch * pixels

    def hsum(s):
        return lat_ref[s].astype(F32) + embed_ref[pl.ds(s, 1), :]

    def add_up(s, carry):
        mean_ref[pl.ds(s, 1), :] = jnp.sum(hsum(s), axis=0, keepdims=True)
        return carry

    def add_squares(s, carry):
        diff = hsum(s) - mean_ref[pl.ds(s, 1), :]
        root_ref[pl.ds(s, 1), :] = jnp.sum(diff * diff, axis=0, keepdims=True)
        return carry

    def clear():
        edge = jnp.zeros((count, side, wide), BF16)
        for ref in (taps_ref, shifts_ref):
            ref[:, :side, :] = edge
            ref[:, side + pixels :, :] = edge
        join_sum_ref[...] = jnp.zeros_like(join_sum_ref)

    def statistics():
        lane = lambda axis: lax.broadcasted_iota(jnp.int32, (width, width), axis)
        low = lane(0) * groups // width * per
        same = ((lane(1) >= low) & (lane(1) < low + per)).astype(F32)
        lax.fori_loop(0, count, add_up, 0)
        mean_ref[...] = spread(mean_ref[...], same) * scale
        lax.fori_loop(0, count, add_squares, 0)
        root_ref[...] = 1.0 / jnp.sqrt(spread(root_ref[...], same) * scale + 1e-05)

    def normalize(s, carry):
        normed = (hsum(s) - mean_ref[pl.ds(s, 1), :]) * root_ref[pl.ds(s, 1), :]
        inner = pl.ds(side, pixels)
        taps_ref[s, inner, :width] = shifted_columns(normed, -1, side).astype(BF16)
        taps_ref[s, inner, width : 2 * width] = normed.astype(BF16)
        taps_ref[s, inner, 2 * width :] = shifted_columns(normed, 1, side).astype(BF16)
        flipped_ref[:, pl.ds(pl.multiple_of(s * pixels, pixels), pixels)] = normed.T.astype(BF16)
        return carry

    def through(c, carry):
        some = pl.ds(c * batch, batch)
        conv = None
        for ty in range(3):
            term = jnp.dot(
                taps_ref[some, pl.ds(ty * side, pixels), :].reshape(rows, wide),
                control_ref[pl.ds(ty * wide, wide), :],
                preferred_element_type=F32,
            )
            conv = term if conv is None else conv + term
        sig = jax.nn.sigmoid(conv)
        act = (conv * sig).astype(BF16)
        slope = sig * (1.0 + conv * (1.0 - sig))
        joined = base_ref[some].reshape(rows, width).astype(F32) + jnp.dot(
            act, join_ref[...], preferred_element_type=F32
        )
        sig = jax.nn.sigmoid(joined)
        mixed = (joined * sig).astype(BF16)
        decoded = jnp.dot(mixed, decoder_ref[...], preferred_element_type=F32)
        decoded_ref[some] = decoded.astype(BF16).reshape(batch, pixels, width)
        dmixed = dot(cot_ref[some].reshape(rows, width), decoder_ref[...], (((1,), (1,)), ((), ())))
        djoin = (dmixed * (sig * (1.0 + joined * (1.0 - sig)))).astype(BF16)
        join_sum_ref[...] += dot(act, djoin, (((0,), (0,)), ((), ())))
        dconv = dot(djoin, join_ref[...], (((1,), (1,)), ((), ()))) * slope
        moved = (shifted_columns(dconv, 1, side), dconv, shifted_columns(dconv, -1, side))
        for tx in range(3):
            value = moved[tx].astype(BF16).reshape(batch, pixels, width)
            for first, breadth in CUTS:
                shifts_ref[
                    some, pl.ds(side, pixels), pl.ds(3 * first + tx * breadth, breadth)
                ] = value[:, :, first : first + breadth]
        return carry

    def grads(ty, cut):
        first, breadth = CUTS[cut]
        value = jnp.dot(
            flipped_ref[...],
            shifts_ref[
                :, pl.ds((2 - ty) * side, pixels), pl.ds(3 * first, 3 * breadth)
            ].reshape(count * pixels, 3 * breadth),
            preferred_element_type=F32,
        )
        return [value[:, tx * breadth : (tx + 1) * breadth] for tx in range(3)]

    return clear, statistics, normalize, through, grads


def step_kernel(
    lat_ref, base_ref, cot_ref, embed_ref, control_ref, join_ref, decoder_ref,
    decoded_ref, control_grad_ref, join_grad_ref, *scratch, side, groups,
):
    clear, statistics, normalize, through, grads = math_parts(
        lat_ref, base_ref, cot_ref, embed_ref, control_ref, join_ref, decoder_ref, decoded_ref,
        *scratch[:2], scratch[2], join_grad_ref, *scratch[3:], side=side, groups=groups,
    )
    count, _, width = lat_ref.shape
    clear()
    statistics()
    lax.fori_loop(0, count, normalize, 0)
    lax.fori_loop(0, count // (2 if count % 2 == 0 else 1), through, 0)
    for cut, (first, breadth) in enumerate(CUTS):
        for ty in range(3):
            for tx, value in enumerate(grads(ty, cut)):
                control_grad_ref[
                    pl.ds((ty * 3 + tx) * width, width), pl.ds(first, breadth)
                ] = value


def math_scratch(count, pixels, width, side):
    return [
        pltpu.VMEM((count, pixels + 2 * side, 3 * width), BF16),
        pltpu.VMEM((count, pixels + 2 * side, 3 * width), BF16),
        pltpu.VMEM((width, count * pixels), BF16),
        pltpu.VMEM((count, width), F32),
        pltpu.VMEM((count, width), F32),
    ]


def local_step(lat, base, cot, embed, control, join, decoder, side):
    return pl.pallas_call(
        functools.partial(step_kernel, side=side, groups=NORM_GROUPS),
        out_shape=(
            jax.ShapeDtypeStruct(lat.shape, BF16),
            jax.ShapeDtypeStruct(control.shape, F32),
            jax.ShapeDtypeStruct(join.shape, F32),
        ),
        in_specs=[pl.BlockSpec(memory_space=pltpu.VMEM)] * 7,
        out_specs=[pl.BlockSpec(memory_space=pltpu.VMEM)] * 3,
        scratch_shapes=math_scratch(*lat.shape, side),
        compiler_params=pltpu.CompilerParams(vmem_limit_bytes=VMEM_LIMIT),
        name="local_step",
    )(lat, base, cot, embed, control, join, decoder)


def ring_kernel(
    lat_in, base_in, cot_in, embed_ref, control_in, join_in, decoder_in,
    decoded_out, control_out, join_out, control_all, join_all,
    lat_ref, base_ref, cot_ref, control_ref, join_ref, decoder_ref, decoded_ref,
    taps_ref, shifts_ref, flipped_ref, mean_ref, root_ref,
    join_sum, grad_a, grad_b,
    a_twin, b_twin, j_twin, a_mine, b_mine, j_mine,
    a_send, b_send, j_send, a_recv, b_recv, j_recv,
    local_sems, out_sems, gather_sends, gather_recvs, sends, recvs,
    *, side, groups,
):
    clear, statistics, normalize, through, grads = math_parts(
        lat_ref, base_ref, cot_ref, embed_ref, control_ref, join_ref, decoder_ref, decoded_ref,
        taps_ref, shifts_ref, flipped_ref, join_sum, mean_ref, root_ref,
        side=side, groups=groups,
    )
    count, _, width = lat_ref.shape
    shard, join_shard = control_in.shape[0], join_in.shape[0]
    me, spot, core = ring_place()
    ahead = dp_index((spot + 1) % 8, core)
    behind = dp_index((spot + 7) % 8, core)
    twin = dp_index(spot, 1 - core)

    load = {}
    for place, (name, src, dst) in enumerate(
        (
            ("lat", lat_in, lat_ref),
            ("base", base_in, base_ref),
            ("cot", cot_in, cot_ref),
            ("decoder", decoder_in, decoder_ref),
            ("own", control_in, control_all.at[pl.ds(pl.multiple_of(me * shard, 8), shard)]),
            ("ownj", join_in, join_all.at[pl.ds(pl.multiple_of(me * join_shard, 8), join_shard)]),
            ("control", control_all, control_ref),
            ("join", join_all, join_ref),
        )
    ):
        load[name] = pltpu.make_async_copy(src, dst, local_sems.at[place])
    load["lat"].start()
    greet((ahead, behind, twin))

    cut_at = (shard // 2 + 7) // 8 * 8
    pieces = (
        (control_in, control_all, shard, 0, cut_at),
        (control_in, control_all, shard, cut_at, shard - cut_at),
        (join_in, join_all, join_shard, 0, join_shard),
    )
    gathered = []

    def lot(piece, block):
        _, whole, size, first, length = pieces[piece]
        return whole.at[pl.ds(pl.multiple_of(block * size + first, 8), length)]

    def give(piece, block, kind, partner, own=False):
        source, _, _, first, length = pieces[piece]
        copy = remote(
            source.at[pl.ds(first, length)] if own else lot(piece, block),
            lot(piece, block), gather_sends, gather_recvs, piece * 15 + kind, partner,
        )
        copy.start()
        gathered.append(copy)

    def arrived(piece, block, kind):
        place = lot(piece, block)
        remote(place, place, gather_sends, gather_recvs, piece * 15 + kind, twin).wait_recv()

    for piece in range(3):
        give(piece, me, 0, ahead, True)
        give(piece, me, 4, behind, True)
    for piece in range(3):
        give(piece, me, 7, twin, True)
    for name in ("own", "ownj", "base", "cot", "decoder"):
        load[name].start()

    def gather_step(step):
        up = dp_index((spot + 7 - step) % 8, core)
        down = dp_index((spot + 1 + step) % 8, core)
        for piece in range(3):
            arrived(piece, up, step)
            if step < 3:
                give(piece, up, step + 1, ahead)
            give(piece, up, 8 + step, twin)
            if step < 3:
                arrived(piece, down, 4 + step)
                if step < 2:
                    give(piece, down, 5 + step, behind)
                give(piece, down, 12 + step, twin)

    clear()
    load["lat"].wait()
    statistics()
    gather_step(0)
    lax.fori_loop(0, count // 2, normalize, 0)
    gather_step(1)
    lax.fori_loop(count // 2, count, normalize, 0)
    gather_step(2)
    gather_step(3)
    for name in ("own", "ownj", "base", "cot", "decoder"):
        load[name].wait()
    for piece in range(3):
        arrived(piece, dp_index(spot, 1 - core), 7)
        for step in range(4):
            arrived(piece, dp_index((spot + 7 - step) % 8, 1 - core), 8 + step)
        for step in range(3):
            arrived(piece, dp_index((spot + 1 + step) % 8, 1 - core), 12 + step)
    for name in ("control", "join"):
        load[name].start()
    for copy in gathered:
        copy.wait_send()
    for name in ("control", "join"):
        load[name].wait()

    lax.fori_loop(0, count // 2, through, 0)
    result = pltpu.make_async_copy(decoded_ref, decoded_out, out_sems.at[0])
    result.start()

    arrays = (
        (grad_a, a_mine, a_twin, a_send, a_recv, shard),
        (grad_b, b_mine, b_twin, b_send, b_recv, shard),
        (join_sum, j_mine, j_twin, j_send, j_recv, join_shard),
    )
    started = []

    def part_of(which, k, lane):
        part, size = arrays[which][0], arrays[which][5]
        block = dp_index((spot + k) % 8, lane)
        return part[pl.ds(pl.multiple_of(block * size, 8), size), :]

    def to_twin(which):
        mine, held = arrays[which][1], arrays[which][2]
        for k in (4, 5, 3, 6, 2, 7, 1, 0):
            mine[k] = part_of(which, k, 1 - core).astype(BF16)
            copy = remote(
                mine.at[k], held.at[k], sends, recvs, which * 15 + 7 + k, twin
            )
            copy.start()
            started.append(copy)

    def pair_sum(which, k):
        held = arrays[which][2]
        remote(held.at[k], held.at[k], sends, recvs, which * 15 + 7 + k, twin).wait_recv()
        return part_of(which, k, core) + held[k].astype(F32)

    def got(which, place):
        back = arrays[which][4]
        remote(back.at[place], back.at[place], sends, recvs, which * 15 + place, twin).wait_recv()
        return back[place].astype(F32)

    def hop(which, place, value, partner):
        out, back = arrays[which][3], arrays[which][4]
        out[place] = value.astype(BF16)
        copy = remote(out.at[place], back.at[place], sends, recvs, which * 15 + place, partner)
        copy.start()
        started.append(copy)

    def ring_step(which, step):
        value = pair_sum(which, 4 - step)
        hop(which, step, value + got(which, step - 1) if step > 0 else value, ahead)
        if step < 3:
            value = pair_sum(which, 5 + step)
            hop(which, 4 + step, value + got(which, 3 + step) if step > 0 else value, behind)

    def finish(which):
        return pair_sum(which, 0) + got(which, 6) + got(which, 3)

    def store_grads(ty, cut):
        for tx, value in enumerate(grads(ty, cut)):
            arrays[cut][0][pl.ds((ty * 3 + tx) * width, width), :] = value

    to_twin(2)
    for ty in range(3):
        store_grads(ty, 0)
    to_twin(0)
    store_grads(0, 1)
    ring_step(0, 0)
    ring_step(2, 0)
    store_grads(1, 1)
    store_grads(2, 1)
    to_twin(1)
    ring_step(0, 1)
    ring_step(1, 0)
    ring_step(2, 1)
    for step in (2, 3):
        ring_step(0, step)
        ring_step(1, step - 1)
        ring_step(2, step)
    control_out[:, pl.ds(0, CUTS[0][1])] = finish(0)
    ring_step(1, 3)
    join_out[...] = finish(2)
    control_out[:, pl.ds(*CUTS[1])] = finish(1)
    for copy in started:
        copy.wait_send()
    result.wait()


def ring_step_call(lat, base, cot, embed, control, join, decoder, side):
    count, pixels, width = lat.shape
    shard, join_shard = control.shape[0], join.shape[0]
    whole = (16 * shard, width)
    blocks = [(shard, CUTS[0][1]), (shard, CUTS[1][1]), (join_shard, width)]
    anywhere = pl.BlockSpec(memory_space=pl.ANY)
    held = pl.BlockSpec(memory_space=pltpu.VMEM)
    outs = pl.pallas_call(
        functools.partial(ring_kernel, side=side, groups=NORM_GROUPS),
        out_shape=(
            jax.ShapeDtypeStruct(lat.shape, BF16),
            jax.ShapeDtypeStruct(control.shape, F32),
            jax.ShapeDtypeStruct(join.shape, F32),
            jax.ShapeDtypeStruct(whole, BF16),
            jax.ShapeDtypeStruct((16 * join_shard, width), BF16),
        ),
        in_specs=[anywhere, anywhere, anywhere, held, anywhere, anywhere, anywhere],
        out_specs=[anywhere, held, held, anywhere, anywhere],
        scratch_shapes=[
            pltpu.VMEM(lat.shape, BF16),
            pltpu.VMEM(lat.shape, BF16),
            pltpu.VMEM(lat.shape, BF16),
            pltpu.VMEM(whole, BF16),
            pltpu.VMEM((16 * join_shard, width), BF16),
            pltpu.VMEM(decoder.shape, BF16),
            pltpu.VMEM(lat.shape, BF16),
        ]
        + math_scratch(count, pixels, width, side)
        + [pltpu.VMEM((width, width), F32)]
        + [pltpu.VMEM((whole[0], breadth), F32) for _, breadth in CUTS]
        + [pltpu.VMEM((slots,) + block, BF16) for slots in (8, 8, 7, 7) for block in blocks]
        + [
            pltpu.SemaphoreType.DMA((slots,)) for slots in (8, 1, 45, 45, 45, 45)
        ],
        compiler_params=pltpu.CompilerParams(
            collective_id=0, has_side_effects=True, vmem_limit_bytes=VMEM_LIMIT
        ),
        name="ring_step",
    )(lat, base, cot, embed, control, join, decoder)
    return outs[:3]


def on_device(
    ringed, latents, base_features, cotangent, class_ids, timesteps,
    class_table, control_weight, join_weight, decoder_weight,
):
    count, side, _, width = latents.shape
    flat = lambda array: array.reshape(count, side * side, width)
    embed = class_table.at[class_ids].get(mode="promise_in_bounds") + time_features(
        timesteps, width
    )
    maps = (flat(latents), flat(base_features), flat(cotangent), embed)
    if ringed:
        decoded, control_grad, join_grad = ring_step_call(
            *maps, control_weight, join_weight, decoder_weight, side
        )
        return decoded.reshape(latents.shape), control_grad, join_grad
    control_full, join_full = (
        lax.all_gather(weight, "dp", axis=0, tiled=True) for weight in (control_weight, join_weight)
    )
    decoded, control_part, join_part = local_step(
        *maps, control_full, join_full, decoder_weight, side
    )
    control_grad, join_grad = (
        lax.psum_scatter(part, "dp", scatter_dimension=0, tiled=True)
        for part in (control_part, join_part)
    )
    return decoded.reshape(latents.shape), control_grad, join_grad


def solution(mesh):
    rows = P(("groups", "dp"), None)
    maps = P(("groups", "dp"), None, None, None)
    each = P(("groups", "dp"))
    split = P("dp", None)
    ringed = mesh.shape["dp"] == 16
    return jax.shard_map(
        functools.partial(on_device, ringed),
        mesh=mesh,
        in_specs=(maps, maps, maps, each, each, P(), split, split, P()),
        out_specs=(maps, rows, rows),
        check_vma=False,
    )
```

```python
import functools
import math

import jax
import jax.numpy as jnp
import numpy as np
from jax import lax
from jax.experimental import pallas as pl
from jax.experimental.pallas import tpu as pltpu
from jax.sharding import PartitionSpec as P

NORM_GROUPS = 32
MESH = pl.DeviceIdType.MESH
F32 = jnp.float32
BF16 = jnp.bfloat16
VMEM_LIMIT = 60000 * 1024


def time_features(steps_in, width):
    half = width // 2
    freq = jnp.exp(-math.log(10000.0) * jnp.arange(half, dtype=jnp.float32) / half)
    angle = steps_in.astype(jnp.float32)[:, None] * freq[None, :]
    return jnp.concatenate([jnp.cos(angle), jnp.sin(angle)], axis=1)


def silu_slope(value):
    sig = jax.nn.sigmoid(value)
    return sig * (1.0 + value * (1.0 - sig))


def dp_index(spot, core):
    y = spot // 4
    z = spot + y * (7 - 2 * spot)
    return z * 4 + y * 2 + core


def ring_place():
    me = lax.axis_index("dp")
    z, y, core = me // 4, (me // 2) % 2, me % 2
    return me, z + y * (7 - 2 * z), core


def greet(partners):
    barrier = pltpu.get_barrier_semaphore()
    for partner in partners:
        pl.semaphore_signal(barrier, inc=1, device_id={"dp": partner}, device_id_type=MESH)
    pl.semaphore_wait(barrier, len(partners))


def remote(src, dst, sends, recvs, place, partner):
    return pltpu.make_async_remote_copy(
        src_ref=src,
        dst_ref=dst,
        send_sem=sends.at[place],
        recv_sem=recvs.at[place],
        device_id={"dp": partner},
        device_id_type=MESH,
    )


def shifted_columns(value, step, side):
    rows = value.shape[0]
    spot = lax.broadcasted_iota(jnp.int32, value.shape, 0) % side
    if step > 0:
        return jnp.where(spot == side - 1, 0.0, pltpu.roll(value, rows - 1, 0))
    return jnp.where(spot == 0, 0.0, pltpu.roll(value, 1, 0))


CUTS = ((0, 256), (256, 128))


def math_parts(
    lat_ref, base_ref, cot_ref, embed_ref, control_ref, join_ref, decoder_ref, mixed_ref,
    taps_ref, shifts_ref, flipped_ref, join_sum_ref, mean_ref, root_ref, pulled_ref,
    *, side, groups,
):
    count, pixels, width = lat_ref.shape
    batch = 2 if count % 2 == 0 else 1
    per = width // groups
    spread = functools.partial(
        jnp.dot, precision=lax.Precision.HIGHEST, preferred_element_type=F32
    )
    scale = 1.0 / (pixels * per)
    dot = functools.partial(lax.dot_general, preferred_element_type=F32)
    wide = 3 * width
    rows = batch * pixels

    def hsum(s):
        return lat_ref[s].astype(F32) + embed_ref[pl.ds(s, 1), :]

    def add_up(s, carry):
        mean_ref[pl.ds(s, 1), :] = jnp.sum(hsum(s), axis=0, keepdims=True)
        return carry

    def add_squares(s, carry):
        diff = hsum(s) - mean_ref[pl.ds(s, 1), :]
        root_ref[pl.ds(s, 1), :] = jnp.sum(diff * diff, axis=0, keepdims=True)
        return carry

    def clear():
        edge = jnp.zeros((count, side, wide), BF16)
        for ref in (taps_ref, shifts_ref):
            ref[:, :side, :] = edge
            ref[:, side + pixels :, :] = edge
        join_sum_ref[...] = jnp.zeros_like(join_sum_ref)

    def statistics():
        lane = lambda axis: lax.broadcasted_iota(jnp.int32, (width, width), axis)
        low = lane(0) * groups // width * per
        same = ((lane(1) >= low) & (lane(1) < low + per)).astype(F32)
        lax.fori_loop(0, count, add_up, 0)
        mean_ref[...] = spread(mean_ref[...], same) * scale
        lax.fori_loop(0, count, add_squares, 0)
        root_ref[...] = 1.0 / jnp.sqrt(spread(root_ref[...], same) * scale + 1e-05)

    def normalize(s, carry):
        normed = (hsum(s) - mean_ref[pl.ds(s, 1), :]) * root_ref[pl.ds(s, 1), :]
        inner = pl.ds(side, pixels)
        taps_ref[s, inner, :width] = shifted_columns(normed, -1, side).astype(BF16)
        taps_ref[s, inner, width : 2 * width] = normed.astype(BF16)
        taps_ref[s, inner, 2 * width :] = shifted_columns(normed, 1, side).astype(BF16)
        flipped_ref[:, pl.ds(pl.multiple_of(s * pixels, pixels), pixels)] = normed.T.astype(BF16)
        return carry

    def pull(c, carry):
        some = pl.ds(c * batch, batch)
        pulled_ref[some] = dot(
            cot_ref[some].reshape(rows, width), decoder_ref[...], (((1,), (1,)), ((), ()))
        ).reshape(batch, pixels, width)
        return carry

    def through(c, carry):
        some = pl.ds(c * batch, batch)
        conv = None
        for ty in range(3):
            term = jnp.dot(
                taps_ref[some, pl.ds(ty * side, pixels), :].reshape(rows, wide),
                control_ref[pl.ds(ty * wide, wide), :],
                preferred_element_type=F32,
            )
            conv = term if conv is None else conv + term
        sig = jax.nn.sigmoid(conv)
        act = (conv * sig).astype(BF16)
        slope = sig * (1.0 + conv * (1.0 - sig))
        joined = base_ref[some].reshape(rows, width).astype(F32) + jnp.dot(
            act, join_ref[...], preferred_element_type=F32
        )
        sig = jax.nn.sigmoid(joined)
        mixed_ref[some] = (joined * sig).astype(BF16).reshape(batch, pixels, width)
        djoin = (pulled_ref[some].reshape(rows, width) * (sig * (1.0 + joined * (1.0 - sig)))).astype(BF16)
        join_sum_ref[...] += dot(act, djoin, (((0,), (0,)), ((), ())))
        dconv = dot(djoin, join_ref[...], (((1,), (1,)), ((), ()))) * slope
        moved = (shifted_columns(dconv, 1, side), dconv, shifted_columns(dconv, -1, side))
        for tx in range(3):
            value = moved[tx].astype(BF16).reshape(batch, pixels, width)
            for first, breadth in CUTS:
                shifts_ref[
                    some, pl.ds(side, pixels), pl.ds(3 * first + tx * breadth, breadth)
                ] = value[:, :, first : first + breadth]
        return carry

    def grads(ty, cut):
        first, breadth = CUTS[cut]
        value = jnp.dot(
            flipped_ref[...],
            shifts_ref[
                :, pl.ds((2 - ty) * side, pixels), pl.ds(3 * first, 3 * breadth)
            ].reshape(count * pixels, 3 * breadth),
            preferred_element_type=F32,
        )
        return [value[:, tx * breadth : (tx + 1) * breadth] for tx in range(3)]

    return clear, statistics, normalize, pull, through, grads


def step_kernel(
    lat_ref, base_ref, cot_ref, embed_ref, control_ref, join_ref, decoder_ref,
    mixed_ref, control_grad_ref, join_grad_ref, *scratch, side, groups,
):
    clear, statistics, normalize, pull, through, grads = math_parts(
        lat_ref, base_ref, cot_ref, embed_ref, control_ref, join_ref, decoder_ref, mixed_ref,
        *scratch[:2], scratch[2], join_grad_ref, *scratch[3:], side=side, groups=groups,
    )
    count, _, width = lat_ref.shape
    clear()
    statistics()
    lax.fori_loop(0, count, normalize, 0)
    steps = count // (2 if count % 2 == 0 else 1)
    lax.fori_loop(0, steps, pull, 0)
    lax.fori_loop(0, steps, through, 0)
    for cut, (first, breadth) in enumerate(CUTS):
        for ty in range(3):
            for tx, value in enumerate(grads(ty, cut)):
                control_grad_ref[
                    pl.ds((ty * 3 + tx) * width, width), pl.ds(first, breadth)
                ] = value


def math_scratch(count, pixels, width, side):
    return [
        pltpu.VMEM((count, pixels + 2 * side, 3 * width), BF16),
        pltpu.VMEM((count, pixels + 2 * side, 3 * width), BF16),
        pltpu.VMEM((width, count * pixels), BF16),
        pltpu.VMEM((count, width), F32),
        pltpu.VMEM((count, width), F32),
        pltpu.VMEM((count, pixels, width), F32),
    ]


def local_step(lat, base, cot, embed, control, join, decoder, side):
    return pl.pallas_call(
        functools.partial(step_kernel, side=side, groups=NORM_GROUPS),
        out_shape=(
            jax.ShapeDtypeStruct(lat.shape, BF16),
            jax.ShapeDtypeStruct(control.shape, F32),
            jax.ShapeDtypeStruct(join.shape, F32),
        ),
        in_specs=[pl.BlockSpec(memory_space=pltpu.VMEM)] * 7,
        out_specs=[pl.BlockSpec(memory_space=pltpu.VMEM)] * 3,
        scratch_shapes=math_scratch(*lat.shape, side),
        compiler_params=pltpu.CompilerParams(vmem_limit_bytes=VMEM_LIMIT),
        name="local_step",
    )(lat, base, cot, embed, control, join, decoder)


def ring_kernel(
    ids_ref, times_ref, freq_ref, table_in,
    lat_in, base_in, cot_in, control_in, join_in, decoder_in,
    mixed_out, control_out, join_out, control_all, join_all,
    lat_ref, base_ref, cot_ref, control_ref, join_ref, decoder_ref, mixed_ref,
    table_ref, embed_ref,
    taps_ref, shifts_ref, flipped_ref, mean_ref, root_ref, pulled_ref,
    join_sum, grad_a, grad_b,
    a_twin, b_twin, j_twin, a_mine, b_mine, j_mine,
    a_send, b_send, j_send, a_recv, b_recv, j_recv,
    local_sems, out_sems, gather_sends, gather_recvs, sends, recvs,
    *, side, groups,
):
    clear, statistics, normalize, pull, through, grads = math_parts(
        lat_ref, base_ref, cot_ref, embed_ref, control_ref, join_ref, decoder_ref, mixed_ref,
        taps_ref, shifts_ref, flipped_ref, join_sum, mean_ref, root_ref, pulled_ref,
        side=side, groups=groups,
    )
    count, _, width = lat_ref.shape
    shard, join_shard = control_in.shape[0], join_in.shape[0]
    me, spot, core = ring_place()
    ahead = dp_index((spot + 1) % 8, core)
    behind = dp_index((spot + 7) % 8, core)
    twin = dp_index(spot, 1 - core)

    load = {}
    for place, (name, src, dst) in enumerate(
        (
            ("lat", lat_in, lat_ref),
            ("base", base_in, base_ref),
            ("cot", cot_in, cot_ref),
            ("decoder", decoder_in, decoder_ref),
            ("own", control_in, control_all.at[pl.ds(pl.multiple_of(me * shard, 8), shard)]),
            ("ownj", join_in, join_all.at[pl.ds(pl.multiple_of(me * join_shard, 8), join_shard)]),
            ("control", control_all, control_ref),
            ("join", join_all, join_ref),
            ("table", table_in, table_ref),
        )
    ):
        load[name] = pltpu.make_async_copy(src, dst, local_sems.at[place])
    plane = lax.axis_index("groups")
    load["table"].start()
    load["lat"].start()
    barrier = pltpu.get_barrier_semaphore()
    across = {"groups": 1 - plane, "dp": me}
    for place in ({"dp": ahead}, {"dp": behind}, {"dp": twin}, across):
        pl.semaphore_signal(barrier, inc=1, device_id=place, device_id_type=MESH)
    pl.semaphore_wait(barrier, 4)

    third = shard // 24 * 8
    rest = shard - 2 * third
    pieces = (
        (control_in, control_all, shard, plane * (shard - third), third),
        (control_in, control_all, shard, third, rest),
        (join_in, join_all, join_shard, 0, join_shard),
        (control_in, control_all, shard, (1 - plane) * (shard - third), third),
    )
    gathered = []
    turn = (1, -1, -1)

    def lot(piece, block):
        _, whole, size, first, length = pieces[piece]
        return whole.at[pl.ds(pl.multiple_of(block * size + first, 8), length)]

    def give(piece, block, kind, partner, own=False, sems=None):
        source, _, _, first, length = pieces[piece]
        place = (piece if sems is None else sems) * 15 + kind
        copy = pltpu.make_async_remote_copy(
            src_ref=source.at[pl.ds(pl.multiple_of(first, 8), length)] if own else lot(piece, block),
            dst_ref=lot(piece, block),
            send_sem=gather_sends.at[place],
            recv_sem=gather_recvs.at[place],
            device_id=partner if isinstance(partner, dict) else {"dp": partner},
            device_id_type=MESH,
        )
        copy.start()
        gathered.append(copy)

    def arrived(piece, block, kind):
        place = lot(piece, block)
        remote(place, place, gather_sends, gather_recvs, piece * 15 + kind, twin).wait_recv()

    def source_of(piece, kind, lane):
        away = -(kind + 1) if kind < 4 else kind - 3
        return dp_index((spot + 8 + away * turn[piece % 3]) % 8, lane)

    def way(piece, kind):
        return ahead if (kind < 4) == (turn[piece] == 1) else behind

    for piece in range(3):
        give(piece, me, 0, way(piece, 0), True)
        give(piece, me, 4, way(piece, 4), True)
    for piece in range(4):
        give(piece, me, 7, twin, True)
    for name in ("own", "ownj", "cot", "decoder", "base"):
        load[name].start()

    def pass_on(piece, kind):
        block = source_of(piece, kind, core)
        arrived(piece, block, kind)
        if kind not in (3, 6):
            give(piece, block, kind + 1, way(piece, kind))
        if piece == 0:
            give(0, block, kind, across, sems=3)
        give(piece, block, 8 + kind, twin)

    def gather_step(step):
        for kind in (step, 4 + step) if step < 3 else (step,):
            for piece in range(3):
                pass_on(piece, kind)

    def cross_step(step):
        for kind in (step, 4 + step) if step < 3 else (step,):
            block = source_of(3, kind, core)
            arrived(3, block, kind)
            give(3, block, 8 + kind, twin)

    clear()
    load["table"].wait()
    half = lax.broadcasted_iota(jnp.int32, (1, width), 1) < width // 2
    for s in range(count):
        angle = times_ref[s].astype(F32) * freq_ref[...]
        embed_ref[pl.ds(s, 1), :] = table_ref[pl.ds(ids_ref[s], 1), :] + jnp.where(
            half, jnp.cos(angle), jnp.sin(angle)
        )
    load["lat"].wait()
    statistics()
    gather_step(0)
    lax.fori_loop(0, count // 2, normalize, 0)
    gather_step(1)
    cross_step(0)
    lax.fori_loop(count // 2, count, normalize, 0)
    gather_step(2)
    cross_step(1)
    for name in ("own", "ownj", "cot", "decoder", "base"):
        load[name].wait()
    lax.fori_loop(0, count // 2, pull, 0)
    gather_step(3)
    cross_step(2)
    cross_step(3)
    for piece in range(4):
        arrived(piece, dp_index(spot, 1 - core), 7)
        for kind in range(7):
            arrived(piece, source_of(piece, kind, 1 - core), 8 + kind)
    for name in ("control", "join"):
        load[name].start()
    for copy in gathered:
        copy.wait_send()
    for name in ("control", "join"):
        load[name].wait()

    lax.fori_loop(0, count // 2, through, 0)
    result = pltpu.make_async_copy(mixed_ref, mixed_out, out_sems.at[0])
    result.start()

    arrays = (
        (grad_a, a_mine, a_twin, a_send, a_recv, shard),
        (grad_b, b_mine, b_twin, b_send, b_recv, shard),
        (join_sum, j_mine, j_twin, j_send, j_recv, join_shard),
    )
    started = []

    def part_of(which, k, lane):
        part, size = arrays[which][0], arrays[which][5]
        block = dp_index((spot + k) % 8, lane)
        return part[pl.ds(pl.multiple_of(block * size, 8), size), :]

    def to_twin(which):
        mine, held = arrays[which][1], arrays[which][2]
        for k in (4, 5, 3, 6, 2, 7, 1, 0):
            mine[k] = part_of(which, k, 1 - core).astype(BF16)
            copy = remote(
                mine.at[k], held.at[k], sends, recvs, which * 15 + 7 + k, twin
            )
            copy.start()
            started.append(copy)

    def pair_sum(which, k):
        held = arrays[which][2]
        remote(held.at[k], held.at[k], sends, recvs, which * 15 + 7 + k, twin).wait_recv()
        return part_of(which, k, core) + held[k].astype(F32)

    def got(which, place):
        back = arrays[which][4]
        remote(back.at[place], back.at[place], sends, recvs, which * 15 + place, twin).wait_recv()
        return back[place].astype(F32)

    def hop(which, place, value, partner):
        out, back = arrays[which][3], arrays[which][4]
        out[place] = value.astype(BF16)
        copy = remote(out.at[place], back.at[place], sends, recvs, which * 15 + place, partner)
        copy.start()
        started.append(copy)

    def ring_step(which, step):
        turned = which == 1
        value = pair_sum(which, 4 + step if turned else 4 - step)
        hop(
            which, step, value + got(which, step - 1) if step > 0 else value,
            behind if turned else ahead,
        )
        if step < 3:
            value = pair_sum(which, 3 - step if turned else 5 + step)
            hop(
                which, 4 + step, value + got(which, 3 + step) if step > 0 else value,
                ahead if turned else behind,
            )

    def finish(which):
        return pair_sum(which, 0) + got(which, 6) + got(which, 3)

    def store_grads(ty, cut):
        for tx, value in enumerate(grads(ty, cut)):
            arrays[cut][0][pl.ds((ty * 3 + tx) * width, width), :] = value

    to_twin(2)
    for ty in range(3):
        store_grads(ty, 0)
    to_twin(0)
    store_grads(0, 1)
    ring_step(0, 0)
    ring_step(2, 0)
    store_grads(1, 1)
    store_grads(2, 1)
    to_twin(1)
    ring_step(0, 1)
    ring_step(1, 0)
    ring_step(2, 1)
    for step in (2, 3):
        ring_step(0, step)
        ring_step(1, step - 1)
        ring_step(2, step)
    control_out[:, pl.ds(0, CUTS[0][1])] = finish(0)
    ring_step(1, 3)
    join_out[...] = finish(2)
    control_out[:, pl.ds(*CUTS[1])] = finish(1)
    for copy in started:
        copy.wait_send()
    result.wait()


def ring_step_call(ids, times, freq, table, lat, base, cot, control, join, decoder, side):
    count, pixels, width = lat.shape
    shard, join_shard = control.shape[0], join.shape[0]
    whole = (16 * shard, width)
    blocks = [(shard, CUTS[0][1]), (shard, CUTS[1][1]), (join_shard, width)]
    anywhere = pl.BlockSpec(memory_space=pl.ANY)
    held = pl.BlockSpec(memory_space=pltpu.VMEM)
    outs = pl.pallas_call(
        functools.partial(ring_kernel, side=side, groups=NORM_GROUPS),
        out_shape=(
            jax.ShapeDtypeStruct(lat.shape, BF16),
            jax.ShapeDtypeStruct(control.shape, F32),
            jax.ShapeDtypeStruct(join.shape, F32),
            jax.ShapeDtypeStruct(whole, BF16),
            jax.ShapeDtypeStruct((16 * join_shard, width), BF16),
        ),
        in_specs=[pl.BlockSpec(memory_space=pltpu.SMEM)] * 2 + [held] + [anywhere] * 7,
        out_specs=[anywhere, held, held, anywhere, anywhere],
        scratch_shapes=[
            pltpu.VMEM(lat.shape, BF16),
            pltpu.VMEM(lat.shape, BF16),
            pltpu.VMEM(lat.shape, BF16),
            pltpu.VMEM(whole, BF16),
            pltpu.VMEM((16 * join_shard, width), BF16),
            pltpu.VMEM(decoder.shape, BF16),
            pltpu.VMEM(lat.shape, BF16),
            pltpu.VMEM(table.shape, F32),
            pltpu.VMEM((count, width), F32),
        ]
        + math_scratch(count, pixels, width, side)
        + [pltpu.VMEM((width, width), F32)]
        + [pltpu.VMEM((whole[0], breadth), F32) for _, breadth in CUTS]
        + [pltpu.VMEM((slots,) + block, BF16) for slots in (8, 8, 7, 7) for block in blocks]
        + [
            pltpu.SemaphoreType.DMA((slots,)) for slots in (9, 1, 60, 60, 45, 45)
        ],
        compiler_params=pltpu.CompilerParams(
            collective_id=0, has_side_effects=True, vmem_limit_bytes=VMEM_LIMIT
        ),
        name="ring_step",
    )(ids, times, freq, table, lat, base, cot, control, join, decoder)
    return outs[:3]


def decode_kernel(mixed_ref, decoder_ref, g_ref, j_ref, decoded_ref, g_out, j_out):
    batch, pixels, width = mixed_ref.shape
    decoded_ref[...] = (
        jnp.dot(
            mixed_ref[...].reshape(batch * pixels, width),
            decoder_ref[...],
            preferred_element_type=F32,
        )
        .astype(BF16)
        .reshape(batch, pixels, width)
    )

    @pl.when(pl.program_id(0) == 0)
    def _():
        g_out[...] = g_ref[...]
        j_out[...] = j_ref[...]


def decode(mixed, decoder, g, j):
    count, pixels, width = mixed.shape
    batch = 2 if count % 2 == 0 else 1
    maps = pl.BlockSpec((batch, pixels, width), lambda c: (c, 0, 0))
    fixed = [pl.BlockSpec(array.shape, lambda c: (0, 0)) for array in (decoder, g, j)]
    return pl.pallas_call(
        decode_kernel,
        grid=(count // batch,),
        out_shape=tuple(jax.ShapeDtypeStruct(array.shape, array.dtype) for array in (mixed, g, j)),
        in_specs=[maps] + fixed,
        out_specs=[maps] + fixed[1:],
        name="decode",
    )(mixed, decoder, g, j)


def on_device(
    ringed, latents, base_features, cotangent, class_ids, timesteps,
    class_table, control_weight, join_weight, decoder_weight,
):
    count, side, _, width = latents.shape
    flat = lambda array: array.reshape(count, side * side, width)
    maps = (flat(latents), flat(base_features), flat(cotangent))
    if ringed:
        half = width // 2
        freq = np.exp(-math.log(10000.0) * np.arange(half) / half).astype(np.float32)
        mixed, control_grad, join_grad = ring_step_call(
            class_ids, timesteps, jnp.asarray(np.tile(freq, 2)[None]), class_table,
            *maps, control_weight, join_weight, decoder_weight, side,
        )
        decoded, control_grad, join_grad = decode(
            mixed, decoder_weight, control_grad, join_grad
        )
        return decoded.reshape(latents.shape), control_grad, join_grad
    embed = class_table.at[class_ids].get(mode="promise_in_bounds") + time_features(
        timesteps, width
    )
    control_full, join_full = (
        lax.all_gather(weight, "dp", axis=0, tiled=True) for weight in (control_weight, join_weight)
    )
    mixed, control_part, join_part = local_step(
        *maps, embed, control_full, join_full, decoder_weight, side
    )
    control_grad, join_grad = (
        lax.psum_scatter(part, "dp", scatter_dimension=0, tiled=True)
        for part in (control_part, join_part)
    )
    decoded, control_grad, join_grad = decode(mixed, decoder_weight, control_grad, join_grad)
    return decoded.reshape(latents.shape), control_grad, join_grad


def solution(mesh):
    rows = P(("groups", "dp"), None)
    maps = P(("groups", "dp"), None, None, None)
    each = P(("groups", "dp"))
    split = P("dp", None)
    ringed = dict(mesh.shape) == {"groups": 2, "dp": 16}
    return jax.shard_map(
        functools.partial(on_device, ringed),
        mesh=mesh,
        in_specs=(maps, maps, maps, each, each, P(), split, split, P()),
        out_specs=(maps, rows, rows),
        check_vma=False,
    )
```

```python
import functools
import math

import jax
import jax.numpy as jnp
import numpy as np
from jax import lax
from jax.experimental import pallas as pl
from jax.experimental.pallas import tpu as pltpu
from jax.sharding import PartitionSpec as P

NORM_GROUPS = 32
MESH = pl.DeviceIdType.MESH
F32 = jnp.float32
BF16 = jnp.bfloat16
VMEM_LIMIT = 60000 * 1024


def time_features(steps_in, width):
    half = width // 2
    freq = jnp.exp(-math.log(10000.0) * jnp.arange(half, dtype=jnp.float32) / half)
    angle = steps_in.astype(jnp.float32)[:, None] * freq[None, :]
    return jnp.concatenate([jnp.cos(angle), jnp.sin(angle)], axis=1)


def silu_slope(value):
    sig = jax.nn.sigmoid(value)
    return sig * (1.0 + value * (1.0 - sig))


def dp_index(spot, core):
    y = spot // 4
    z = spot + y * (7 - 2 * spot)
    return z * 4 + y * 2 + core


def ring_place():
    me = lax.axis_index("dp")
    z, y, core = me // 4, (me // 2) % 2, me % 2
    return me, z + y * (7 - 2 * z), core


def greet(partners):
    barrier = pltpu.get_barrier_semaphore()
    for partner in partners:
        pl.semaphore_signal(barrier, inc=1, device_id={"dp": partner}, device_id_type=MESH)
    pl.semaphore_wait(barrier, len(partners))


def remote(src, dst, sends, recvs, place, partner):
    return pltpu.make_async_remote_copy(
        src_ref=src,
        dst_ref=dst,
        send_sem=sends.at[place],
        recv_sem=recvs.at[place],
        device_id={"dp": partner},
        device_id_type=MESH,
    )


def shifted_columns(value, step, side):
    rows = value.shape[0]
    spot = lax.broadcasted_iota(jnp.int32, value.shape, 0) % side
    if step > 0:
        return jnp.where(spot == side - 1, 0.0, pltpu.roll(value, rows - 1, 0))
    return jnp.where(spot == 0, 0.0, pltpu.roll(value, 1, 0))


CUTS = ((0, 256), (256, 128))


def math_parts(
    lat_ref, base_ref, cot_ref, embed_ref, control_ref, join_ref, decoder_ref, mixed_ref,
    taps_ref, shifts_ref, flipped_ref, join_sum_ref, mean_ref, root_ref, pulled_ref,
    *, side, groups,
):
    count, pixels, width = lat_ref.shape
    batch = 2 if count % 2 == 0 else 1
    per = width // groups
    spread = functools.partial(
        jnp.dot, precision=lax.Precision.HIGHEST, preferred_element_type=F32
    )
    scale = 1.0 / (pixels * per)
    dot = functools.partial(lax.dot_general, preferred_element_type=F32)
    wide = 3 * width
    rows = batch * pixels

    def hsum(s):
        return lat_ref[s].astype(F32) + embed_ref[pl.ds(s, 1), :]

    def add_up(s, carry):
        mean_ref[pl.ds(s, 1), :] = jnp.sum(hsum(s), axis=0, keepdims=True)
        return carry

    def add_squares(s, carry):
        diff = hsum(s) - mean_ref[pl.ds(s, 1), :]
        root_ref[pl.ds(s, 1), :] = jnp.sum(diff * diff, axis=0, keepdims=True)
        return carry

    def clear():
        edge = jnp.zeros((count, side, wide), BF16)
        for ref in (taps_ref, shifts_ref):
            ref[:, :side, :] = edge
            ref[:, side + pixels :, :] = edge
        join_sum_ref[...] = jnp.zeros_like(join_sum_ref)

    def statistics():
        lane = lambda axis: lax.broadcasted_iota(jnp.int32, (width, width), axis)
        low = lane(0) * groups // width * per
        same = ((lane(1) >= low) & (lane(1) < low + per)).astype(F32)
        lax.fori_loop(0, count, add_up, 0)
        mean_ref[...] = spread(mean_ref[...], same) * scale
        lax.fori_loop(0, count, add_squares, 0)
        root_ref[...] = 1.0 / jnp.sqrt(spread(root_ref[...], same) * scale + 1e-05)

    def normalize(s, carry):
        normed = (hsum(s) - mean_ref[pl.ds(s, 1), :]) * root_ref[pl.ds(s, 1), :]
        inner = pl.ds(side, pixels)
        taps_ref[s, inner, :width] = shifted_columns(normed, -1, side).astype(BF16)
        taps_ref[s, inner, width : 2 * width] = normed.astype(BF16)
        taps_ref[s, inner, 2 * width :] = shifted_columns(normed, 1, side).astype(BF16)
        flipped_ref[:, pl.ds(pl.multiple_of(s * pixels, pixels), pixels)] = normed.T.astype(BF16)
        return carry

    def pull(c, carry):
        some = pl.ds(c * batch, batch)
        pulled_ref[some] = dot(
            cot_ref[some].reshape(rows, width), decoder_ref[...], (((1,), (1,)), ((), ()))
        ).reshape(batch, pixels, width)
        return carry

    def through(c, carry):
        some = pl.ds(c * batch, batch)
        conv = None
        for ty in range(3):
            term = jnp.dot(
                taps_ref[some, pl.ds(ty * side, pixels), :].reshape(rows, wide),
                control_ref[pl.ds(ty * wide, wide), :],
                preferred_element_type=F32,
            )
            conv = term if conv is None else conv + term
        sig = jax.nn.sigmoid(conv)
        act = (conv * sig).astype(BF16)
        slope = sig * (1.0 + conv * (1.0 - sig))
        joined = base_ref[some].reshape(rows, width).astype(F32) + jnp.dot(
            act, join_ref[...], preferred_element_type=F32
        )
        sig = jax.nn.sigmoid(joined)
        mixed_ref[some] = (joined * sig).astype(BF16).reshape(batch, pixels, width)
        djoin = (pulled_ref[some].reshape(rows, width) * (sig * (1.0 + joined * (1.0 - sig)))).astype(BF16)
        join_sum_ref[...] += dot(act, djoin, (((0,), (0,)), ((), ())))
        dconv = dot(djoin, join_ref[...], (((1,), (1,)), ((), ()))) * slope
        moved = (shifted_columns(dconv, 1, side), dconv, shifted_columns(dconv, -1, side))
        for tx in range(3):
            value = moved[tx].astype(BF16).reshape(batch, pixels, width)
            for first, breadth in CUTS:
                shifts_ref[
                    some, pl.ds(side, pixels), pl.ds(3 * first + tx * breadth, breadth)
                ] = value[:, :, first : first + breadth]
        return carry

    def grads(ty, cut):
        first, breadth = CUTS[cut]
        value = jnp.dot(
            flipped_ref[...],
            shifts_ref[
                :, pl.ds((2 - ty) * side, pixels), pl.ds(3 * first, 3 * breadth)
            ].reshape(count * pixels, 3 * breadth),
            preferred_element_type=F32,
        )
        return [value[:, tx * breadth : (tx + 1) * breadth] for tx in range(3)]

    return clear, statistics, normalize, pull, through, grads


def step_kernel(
    lat_ref, base_ref, cot_ref, embed_ref, control_ref, join_ref, decoder_ref,
    mixed_ref, control_grad_ref, join_grad_ref, *scratch, side, groups,
):
    clear, statistics, normalize, pull, through, grads = math_parts(
        lat_ref, base_ref, cot_ref, embed_ref, control_ref, join_ref, decoder_ref, mixed_ref,
        *scratch[:2], scratch[2], join_grad_ref, *scratch[3:], side=side, groups=groups,
    )
    count, _, width = lat_ref.shape
    clear()
    statistics()
    lax.fori_loop(0, count, normalize, 0)
    steps = count // (2 if count % 2 == 0 else 1)
    lax.fori_loop(0, steps, pull, 0)
    lax.fori_loop(0, steps, through, 0)
    for cut, (first, breadth) in enumerate(CUTS):
        for ty in range(3):
            for tx, value in enumerate(grads(ty, cut)):
                control_grad_ref[
                    pl.ds((ty * 3 + tx) * width, width), pl.ds(first, breadth)
                ] = value


def math_scratch(count, pixels, width, side):
    return [
        pltpu.VMEM((count, pixels + 2 * side, 3 * width), BF16),
        pltpu.VMEM((count, pixels + 2 * side, 3 * width), BF16),
        pltpu.VMEM((width, count * pixels), BF16),
        pltpu.VMEM((count, width), F32),
        pltpu.VMEM((count, width), F32),
        pltpu.VMEM((count, pixels, width), F32),
    ]


def local_step(lat, base, cot, embed, control, join, decoder, side):
    return pl.pallas_call(
        functools.partial(step_kernel, side=side, groups=NORM_GROUPS),
        out_shape=(
            jax.ShapeDtypeStruct(lat.shape, BF16),
            jax.ShapeDtypeStruct(control.shape, F32),
            jax.ShapeDtypeStruct(join.shape, F32),
        ),
        in_specs=[pl.BlockSpec(memory_space=pltpu.VMEM)] * 7,
        out_specs=[pl.BlockSpec(memory_space=pltpu.VMEM)] * 3,
        scratch_shapes=math_scratch(*lat.shape, side),
        compiler_params=pltpu.CompilerParams(vmem_limit_bytes=VMEM_LIMIT),
        name="local_step",
    )(lat, base, cot, embed, control, join, decoder)


def ring_kernel(
    ids_ref, times_ref, freq_ref, table_in,
    lat_in, base_in, cot_in, control_in, join_in, decoder_in,
    mixed_out, control_out, join_out, control_all, join_all,
    lat_ref, base_ref, cot_ref, control_ref, join_ref, decoder_ref, mixed_ref,
    table_ref, embed_ref,
    taps_ref, shifts_ref, flipped_ref, mean_ref, root_ref, pulled_ref,
    join_sum, grad_a, grad_b,
    a_twin, b_twin, j_twin, a_mine, b_mine, j_mine,
    a_send, b_send, j_send, a_recv, b_recv, j_recv,
    local_sems, out_sems, gather_sends, gather_recvs, sends, recvs,
    *, side, groups,
):
    clear, statistics, normalize, pull, through, grads = math_parts(
        lat_ref, base_ref, cot_ref, embed_ref, control_ref, join_ref, decoder_ref, mixed_ref,
        taps_ref, shifts_ref, flipped_ref, join_sum, mean_ref, root_ref, pulled_ref,
        side=side, groups=groups,
    )
    count, _, width = lat_ref.shape
    shard, join_shard = control_in.shape[0], join_in.shape[0]
    me, spot, core = ring_place()
    ahead = dp_index((spot + 1) % 8, core)
    behind = dp_index((spot + 7) % 8, core)
    twin = dp_index(spot, 1 - core)

    load = {}
    for place, (name, src, dst) in enumerate(
        (
            ("lat", lat_in, lat_ref),
            ("base", base_in, base_ref),
            ("cot", cot_in, cot_ref),
            ("decoder", decoder_in, decoder_ref),
            ("own", control_in, control_all.at[pl.ds(pl.multiple_of(me * shard, 8), shard)]),
            ("ownj", join_in, join_all.at[pl.ds(pl.multiple_of(me * join_shard, 8), join_shard)]),
            ("control", control_all, control_ref),
            ("join", join_all, join_ref),
            ("table", table_in, table_ref),
        )
    ):
        load[name] = pltpu.make_async_copy(src, dst, local_sems.at[place])
    plane = lax.axis_index("groups")
    load["table"].start()
    load["lat"].start()
    barrier = pltpu.get_barrier_semaphore()
    across = {"groups": 1 - plane, "dp": me}
    for place in ({"dp": ahead}, {"dp": behind}, {"dp": twin}, across):
        pl.semaphore_signal(barrier, inc=1, device_id=place, device_id_type=MESH)
    pl.semaphore_wait(barrier, 4)

    third = shard // 24 * 8
    rest = shard - 2 * third
    pieces = (
        (control_in, control_all, shard, plane * (shard - third), third),
        (control_in, control_all, shard, third, rest),
        (join_in, join_all, join_shard, 0, join_shard),
        (control_in, control_all, shard, (1 - plane) * (shard - third), third),
    )
    gathered = []
    turn = (1, -1, -1)

    def lot(piece, block):
        _, whole, size, first, length = pieces[piece]
        return whole.at[pl.ds(pl.multiple_of(block * size + first, 8), length)]

    def give(piece, block, kind, partner, own=False, sems=None):
        source, _, _, first, length = pieces[piece]
        place = (piece if sems is None else sems) * 15 + kind
        copy = pltpu.make_async_remote_copy(
            src_ref=source.at[pl.ds(pl.multiple_of(first, 8), length)] if own else lot(piece, block),
            dst_ref=lot(piece, block),
            send_sem=gather_sends.at[place],
            recv_sem=gather_recvs.at[place],
            device_id=partner if isinstance(partner, dict) else {"dp": partner},
            device_id_type=MESH,
        )
        copy.start()
        gathered.append(copy)

    def arrived(piece, block, kind):
        place = lot(piece, block)
        remote(place, place, gather_sends, gather_recvs, piece * 15 + kind, twin).wait_recv()

    def source_of(piece, kind, lane):
        away = -(kind + 1) if kind < 4 else kind - 3
        return dp_index((spot + 8 + away * turn[piece % 3]) % 8, lane)

    def way(piece, kind):
        return ahead if (kind < 4) == (turn[piece] == 1) else behind

    for piece in range(3):
        give(piece, me, 0, way(piece, 0), True)
        give(piece, me, 4, way(piece, 4), True)
    for piece in range(4):
        give(piece, me, 7, twin, True)
    for name in ("own", "ownj", "cot", "decoder", "base"):
        load[name].start()

    def pass_on(piece, kind):
        block = source_of(piece, kind, core)
        arrived(piece, block, kind)
        if kind not in (3, 6):
            give(piece, block, kind + 1, way(piece, kind))
        if piece == 0:
            give(0, block, kind, across, sems=3)
        give(piece, block, 8 + kind, twin)

    def gather_step(step):
        for kind in (step, 4 + step) if step < 3 else (step,):
            for piece in range(3):
                pass_on(piece, kind)

    def cross_step(step):
        for kind in (step, 4 + step) if step < 3 else (step,):
            block = source_of(3, kind, core)
            arrived(3, block, kind)
            give(3, block, 8 + kind, twin)

    clear()
    load["table"].wait()
    half = lax.broadcasted_iota(jnp.int32, (1, width), 1) < width // 2
    for s in range(count):
        angle = times_ref[s].astype(F32) * freq_ref[...]
        embed_ref[pl.ds(s, 1), :] = table_ref[pl.ds(ids_ref[s], 1), :] + jnp.where(
            half, jnp.cos(angle), jnp.sin(angle)
        )
    gather_step(0)
    load["lat"].wait()
    statistics()
    gather_step(1)
    lax.fori_loop(0, count // 2, normalize, 0)
    cross_step(0)
    lax.fori_loop(count // 2, count, normalize, 0)
    gather_step(2)
    cross_step(1)
    for name in ("own", "ownj", "cot", "decoder", "base"):
        load[name].wait()
    lax.fori_loop(0, count // 2, pull, 0)
    gather_step(3)
    cross_step(2)
    cross_step(3)
    for piece in range(4):
        arrived(piece, dp_index(spot, 1 - core), 7)
        for kind in range(7):
            arrived(piece, source_of(piece, kind, 1 - core), 8 + kind)
    for name in ("control", "join"):
        load[name].start()
    for copy in gathered:
        copy.wait_send()
    for name in ("control", "join"):
        load[name].wait()

    lax.fori_loop(0, count // 2, through, 0)
    result = pltpu.make_async_copy(mixed_ref, mixed_out, out_sems.at[0])
    result.start()

    arrays = (
        (grad_a, a_mine, a_twin, a_send, a_recv, shard),
        (grad_b, b_mine, b_twin, b_send, b_recv, shard),
        (join_sum, j_mine, j_twin, j_send, j_recv, join_shard),
    )
    started = []

    def part_of(which, k, lane):
        part, size = arrays[which][0], arrays[which][5]
        block = dp_index((spot + k) % 8, lane)
        return part[pl.ds(pl.multiple_of(block * size, 8), size), :]

    def to_twin(which):
        mine, held = arrays[which][1], arrays[which][2]
        for k in (4, 5, 3, 6, 2, 7, 1, 0):
            mine[k] = part_of(which, k, 1 - core).astype(BF16)
            copy = remote(
                mine.at[k], held.at[k], sends, recvs, which * 15 + 7 + k, twin
            )
            copy.start()
            started.append(copy)

    def pair_sum(which, k):
        held = arrays[which][2]
        remote(held.at[k], held.at[k], sends, recvs, which * 15 + 7 + k, twin).wait_recv()
        return part_of(which, k, core) + held[k].astype(F32)

    def got(which, place):
        back = arrays[which][4]
        remote(back.at[place], back.at[place], sends, recvs, which * 15 + place, twin).wait_recv()
        return back[place].astype(F32)

    def hop(which, place, value, partner):
        out, back = arrays[which][3], arrays[which][4]
        out[place] = value.astype(BF16)
        copy = remote(out.at[place], back.at[place], sends, recvs, which * 15 + place, partner)
        copy.start()
        started.append(copy)

    def ring_step(which, step):
        turned = which == 1
        value = pair_sum(which, 4 + step if turned else 4 - step)
        hop(
            which, step, value + got(which, step - 1) if step > 0 else value,
            behind if turned else ahead,
        )
        if step < 3:
            value = pair_sum(which, 3 - step if turned else 5 + step)
            hop(
                which, 4 + step, value + got(which, 3 + step) if step > 0 else value,
                ahead if turned else behind,
            )

    def finish(which):
        return pair_sum(which, 0) + got(which, 6) + got(which, 3)

    def store_grads(ty, cut):
        for tx, value in enumerate(grads(ty, cut)):
            arrays[cut][0][pl.ds((ty * 3 + tx) * width, width), :] = value

    to_twin(2)
    for ty in range(3):
        store_grads(ty, 0)
    to_twin(0)
    store_grads(0, 1)
    ring_step(0, 0)
    ring_step(2, 0)
    store_grads(1, 1)
    store_grads(2, 1)
    to_twin(1)
    ring_step(0, 1)
    ring_step(1, 0)
    ring_step(2, 1)
    for step in (2, 3):
        ring_step(0, step)
        ring_step(1, step - 1)
        ring_step(2, step)
    control_out[:, pl.ds(0, CUTS[0][1])] = finish(0)
    ring_step(1, 3)
    join_out[...] = finish(2)
    control_out[:, pl.ds(*CUTS[1])] = finish(1)
    for copy in started:
        copy.wait_send()
    result.wait()


def ring_step_call(ids, times, freq, table, lat, base, cot, control, join, decoder, side):
    count, pixels, width = lat.shape
    shard, join_shard = control.shape[0], join.shape[0]
    whole = (16 * shard, width)
    blocks = [(shard, CUTS[0][1]), (shard, CUTS[1][1]), (join_shard, width)]
    anywhere = pl.BlockSpec(memory_space=pl.ANY)
    held = pl.BlockSpec(memory_space=pltpu.VMEM)
    outs = pl.pallas_call(
        functools.partial(ring_kernel, side=side, groups=NORM_GROUPS),
        out_shape=(
            jax.ShapeDtypeStruct(lat.shape, BF16),
            jax.ShapeDtypeStruct(control.shape, F32),
            jax.ShapeDtypeStruct(join.shape, F32),
            jax.ShapeDtypeStruct(whole, BF16),
            jax.ShapeDtypeStruct((16 * join_shard, width), BF16),
        ),
        in_specs=[pl.BlockSpec(memory_space=pltpu.SMEM)] * 2 + [held] + [anywhere] * 7,
        out_specs=[anywhere, held, held, anywhere, anywhere],
        scratch_shapes=[
            pltpu.VMEM(lat.shape, BF16),
            pltpu.VMEM(lat.shape, BF16),
            pltpu.VMEM(lat.shape, BF16),
            pltpu.VMEM(whole, BF16),
            pltpu.VMEM((16 * join_shard, width), BF16),
            pltpu.VMEM(decoder.shape, BF16),
            pltpu.VMEM(lat.shape, BF16),
            pltpu.VMEM(table.shape, F32),
            pltpu.VMEM((count, width), F32),
        ]
        + math_scratch(count, pixels, width, side)
        + [pltpu.VMEM((width, width), F32)]
        + [pltpu.VMEM((whole[0], breadth), F32) for _, breadth in CUTS]
        + [pltpu.VMEM((slots,) + block, BF16) for slots in (8, 8, 7, 7) for block in blocks]
        + [
            pltpu.SemaphoreType.DMA((slots,)) for slots in (9, 1, 60, 60, 45, 45)
        ],
        compiler_params=pltpu.CompilerParams(
            collective_id=0, has_side_effects=True, vmem_limit_bytes=VMEM_LIMIT
        ),
        name="ring_step",
    )(ids, times, freq, table, lat, base, cot, control, join, decoder)
    return outs[:3]


def decode_kernel(mixed_ref, decoder_ref, g_ref, j_ref, decoded_ref, g_out, j_out):
    batch, pixels, width = mixed_ref.shape
    decoded_ref[...] = (
        jnp.dot(
            mixed_ref[...].reshape(batch * pixels, width),
            decoder_ref[...],
            preferred_element_type=F32,
        )
        .astype(BF16)
        .reshape(batch, pixels, width)
    )

    @pl.when(pl.program_id(0) == 0)
    def _():
        g_out[...] = g_ref[...]
        j_out[...] = j_ref[...]


def decode(mixed, decoder, g, j):
    count, pixels, width = mixed.shape
    batch = 2 if count % 2 == 0 else 1
    maps = pl.BlockSpec((batch, pixels, width), lambda c: (c, 0, 0))
    fixed = [pl.BlockSpec(array.shape, lambda c: (0, 0)) for array in (decoder, g, j)]
    return pl.pallas_call(
        decode_kernel,
        grid=(count // batch,),
        out_shape=tuple(jax.ShapeDtypeStruct(array.shape, array.dtype) for array in (mixed, g, j)),
        in_specs=[maps] + fixed,
        out_specs=[maps] + fixed[1:],
        name="decode",
    )(mixed, decoder, g, j)


def on_device(
    ringed, latents, base_features, cotangent, class_ids, timesteps,
    class_table, control_weight, join_weight, decoder_weight,
):
    count, side, _, width = latents.shape
    flat = lambda array: array.reshape(count, side * side, width)
    maps = (flat(latents), flat(base_features), flat(cotangent))
    if ringed:
        half = width // 2
        freq = np.exp(-math.log(10000.0) * np.arange(half) / half).astype(np.float32)
        mixed, control_grad, join_grad = ring_step_call(
            class_ids, timesteps, jnp.asarray(np.tile(freq, 2)[None]), class_table,
            *maps, control_weight, join_weight, decoder_weight, side,
        )
        decoded, control_grad, join_grad = decode(
            mixed, decoder_weight, control_grad, join_grad
        )
        return decoded.reshape(latents.shape), control_grad, join_grad
    embed = class_table.at[class_ids].get(mode="promise_in_bounds") + time_features(
        timesteps, width
    )
    control_full, join_full = (
        lax.all_gather(weight, "dp", axis=0, tiled=True) for weight in (control_weight, join_weight)
    )
    mixed, control_part, join_part = local_step(
        *maps, embed, control_full, join_full, decoder_weight, side
    )
    control_grad, join_grad = (
        lax.psum_scatter(part, "dp", scatter_dimension=0, tiled=True)
        for part in (control_part, join_part)
    )
    decoded, control_grad, join_grad = decode(mixed, decoder_weight, control_grad, join_grad)
    return decoded.reshape(latents.shape), control_grad, join_grad


def solution(mesh):
    rows = P(("groups", "dp"), None)
    maps = P(("groups", "dp"), None, None, None)
    each = P(("groups", "dp"))
    split = P("dp", None)
    ringed = dict(mesh.shape) == {"groups": 2, "dp": 16}
    return jax.shard_map(
        functools.partial(on_device, ringed),
        mesh=mesh,
        in_specs=(maps, maps, maps, each, each, P(), split, split, P()),
        out_specs=(maps, rows, rows),
        check_vma=False,
    )
```
